256 devices in a mesh: rows: 8 (over z), chan: 32 (over y, x, core).
Axes of the slice: x: 4, y: 4, z: 8, core: 2. Of those that a mesh axis runs over, the one named last changes fastest.
Arguments:
- feats: bfloat16 [128, 1024, 1024], P('rows', 'chan'), may hold values from -140 to 140
- norm_gain: float32 [1024], P('chan'), may hold values from 0.1 to 1.9
- proj_weight: float32 [8, 1024], P(None, 'chan'), may hold values from -320 to 320
- chan_bias: float32 [1024], P('chan'), may hold values from -8 to -2
Outputs:
- mixed: bfloat16 [128, 1024, 1024], P('rows', 'chan')
The draws below stay inside these ranges and needn't reach their ends.
All inputs are finite; a program needn't handle non-finite values.
Results may differ from the reference program's by a relative error of at most 0.001.
Values sent between devices are 32-bit elements; how exact they have to be, the bound alone decides.
No kernel may reach another device: no remote copies, remote signals or barrier semaphores. Data moves between devices by JAX's collectives and lax.ppermute only.
A program may use at most 64 MiB of HBM per device.

```python
import jax
import jax.numpy as jnp
from jax import lax

CHANNELS = 1024
COLS = 1024
HEIGHT = 128


def draw_feats(key, part):
    key_jitter = jax.random.fold_in(key, 11)
    key_base = jax.random.fold_in(key, 12)
    full_shape = (HEIGHT, CHANNELS, COLS)
    channel_index = jnp.arange(CHANNELS, dtype=jnp.float32)
    rising = 10.0 ** (channel_index / max(CHANNELS - 1, 1))
    jitter = jax.random.uniform(key_jitter, (CHANNELS,), jnp.float32, 0.8, 1.25)
    channel_scale = (rising * jitter)[None, :, None]
    values = jnp.clip(jax.random.normal(key_base, full_shape, jnp.float32), -6.0, 6.0) * channel_scale
    return values.astype(jnp.bfloat16)


def draw_proj_weight(key, part):
    key_affinity = jax.random.fold_in(key, 21)
    key_gates = jax.random.fold_in(key, 22)
    affinity_normal = jnp.clip(jax.random.normal(key_affinity, (6, CHANNELS), jnp.float32), -4.0, 4.0)
    affinity = affinity_normal * 1.5
    gates = jnp.clip(jax.random.normal(key_gates, (2, CHANNELS), jnp.float32), -4.0, 4.0)
    return jnp.concatenate([affinity, gates], axis=0)


def level_of(stream_key, dims, shards, least, top_value):
    loudness, own = 1.0, jax.random.fold_in(stream_key, 6)
    for axis_at, blocks in shards:
        draws = jnp.exp(jax.random.uniform(jax.random.fold_in(own, axis_at), (blocks,), jnp.float32, least / len(shards), top_value / len(shards)))
        loudness = loudness * jnp.repeat(draws, dims[axis_at] // blocks).reshape([-1 if axis == axis_at else 1 for axis in range(len(dims))])
    return loudness


def setup_inputs(seed: int = 0) -> dict:
    streams_of = jax.random.split(jax.random.key(seed), 5)
    feats = draw_feats(jax.random.fold_in(streams_of[4], 71), 0)
    norm_gain = jnp.clip(1.0 + 0.18 * jax.random.normal(streams_of[1], (CHANNELS,), jnp.float32), 0.1, 1.9)
    proj_weight = draw_proj_weight(jax.random.fold_in(streams_of[4], 71), 0)
    chan_bias = jnp.clip(-8.0 + 6.0 * jax.random.uniform(streams_of[3], (CHANNELS,), jnp.float32) ** level_of(streams_of[3], (CHANNELS,), ((0, 32),), -0.2, 0.2), -8.0, -2.0)
    return {"feats": feats, "norm_gain": norm_gain, "proj_weight": proj_weight, "chan_bias": chan_bias}


EPSILON = 1e-05

def advance(current, row_weights, row_rate):
    edge_zero = jnp.zeros_like(current[:, :1])
    left_side = jnp.concatenate([edge_zero, current[:, :-1]], axis=1)
    right_side = jnp.concatenate([current[:, 1:], edge_zero], axis=1)
    blended = row_weights[0][None, :] * left_side + row_weights[1][None, :] * current + row_weights[2][None, :] * right_side
    return (1.0 - row_rate) * blended

def normalize(feat_row, norm_gain):
    values = feat_row.astype(jnp.float32)
    square_total = lax.optimization_barrier(jnp.sum(values * values, axis=0))
    inverse = 1.0 / jnp.sqrt(square_total / CHANNELS + EPSILON)
    return values * inverse[None, :] * norm_gain[:, None]

def reference(feats, norm_gain, proj_weight, chan_bias):
    logit_scale = CHANNELS ** (-0.5)

    def row_logits(feat_row):
        normed = normalize(feat_row, norm_gain)
        return jnp.dot(proj_weight, normed, precision=lax.Precision.HIGHEST, preferred_element_type=jnp.float32) * logit_scale
    logits = lax.map(row_logits, feats)

    def make_step(offset):

        def row_step(current, inputs):
            feat_row, logit_row = inputs
            row_weights = jax.nn.softmax(logit_row[offset:offset + 3], axis=0)
            row_rate = jax.nn.sigmoid(logit_row[6 + offset // 3][None, :] + chan_bias[:, None])
            current = advance(current, row_weights, row_rate) + jnp.sqrt(row_rate) * normalize(feat_row, norm_gain)
            return (current, current)
        return row_step
    anchor = jnp.zeros((feats.shape[1], feats.shape[2]), jnp.float32)
    _, down_rows = lax.scan(make_step(0), anchor, (feats, logits))
    upward = make_step(3)

    def up_step(current, inputs):
        feat_row, logit_row, down_row = inputs
        current, _ = upward(current, (feat_row, logit_row))
        return (current, (down_row * current).astype(jnp.bfloat16))
    _, output_rows = lax.scan(up_step, anchor, (feats, logits, down_rows), reverse=True)
    return output_rows
```

```python
import jax
import jax.numpy as jnp
from jax import lax
from jax.experimental import pallas as pl
from jax.experimental.pallas import tpu as pltpu
from jax.sharding import PartitionSpec as P

CHANNELS = 1024
EPSILON = 1e-05
LANES = 128
SLOTS = 7

VMEM = pl.BlockSpec(memory_space=pltpu.VMEM)


def call(kernel, outs, *args, aliases=None, limit=40, name=None):
    return pl.pallas_call(
        kernel,
        out_shape=outs,
        in_specs=[VMEM] * len(args),
        out_specs=jax.tree.map(lambda _: VMEM, outs),
        input_output_aliases=aliases or {},
        compiler_params=pltpu.CompilerParams(vmem_limit_bytes=limit << 20),
        name=name,
    )(*args)


def f32(*shape):
    return jax.ShapeDtypeStruct(shape, jnp.float32)


def place():
    chan = lax.axis_index("chan")
    return chan & 1, (chan >> 1) & 3


def lane_tile(core, x):
    return pl.ds(pl.multiple_of((core * 4 + (x & 3)) * LANES, LANES), LANES)


def project(feats, gain, weight, keep, send, wide):
    core, x = place()
    rows, chans, _ = feats.shape
    w, g = weight[...], gain[...]
    picked = [w[0:1] - w[1:2], w[2:3] - w[1:2], w[6:7], w[3:4] - w[4:5], w[5:6] - w[4:5], w[7:8]]
    scaled = [p * g for p in picked]
    depth = rows * chans
    spot = lax.broadcasted_iota(jnp.int32, (chans, depth), 1) % chans
    copies = (spot == lax.broadcasted_iota(jnp.int32, (chans, depth), 0)).astype(jnp.bfloat16)
    band = lax.broadcasted_iota(jnp.int32, (rows, depth), 1) // chans
    own = band == lax.broadcasted_iota(jnp.int32, (rows, depth), 0)
    rest = jnp.concatenate(scaled + scaled[:2], axis=0)
    for part in range(3):
        head = rest.astype(jnp.bfloat16)
        rest = rest - head.astype(jnp.float32)
        spread_out = jnp.dot(head, copies, preferred_element_type=jnp.float32)
        for j in range(6):
            row = jnp.broadcast_to(spread_out[j : j + 1], (rows, depth))
            at = (part * 6 + j) * rows
            wide[at : at + rows] = jnp.where(own, row, 0.0).astype(jnp.bfloat16)
    for half, out in ((0, keep), (1, send)):
        for s in range(4):
            block = feats[:, :, lane_tile(core ^ half, x + s)]
            sums = jnp.dot(wide[...], block.reshape(depth, LANES), preferred_element_type=jnp.float32)
            sums = sums[0 : 6 * rows] + sums[6 * rows : 12 * rows] + sums[12 * rows :]
            out[s, 0:6] = sums.reshape(6, rows, LANES)
            values = block.astype(jnp.float32)
            out[s, 6] = jnp.sum(values * values, axis=1)


def join_cores(keep, arrived, *outs):
    for s, out in enumerate(outs):
        out[...] = keep[s] + arrived[s]


def join_x(a, b, c, d, out):
    out[...] = (a[...] + b[...]) + (c[...] + d[...])


def join_y(a, b, c, d, out):
    total = [(a[j] + b[j]) + (c[j] + d[j]) for j in range(SLOTS)]
    inverse = lax.rsqrt(total[6] / CHANNELS + EPSILON)
    scale = inverse * CHANNELS**-0.5
    for base in (0, 3):
        first, last = total[base] * scale, total[base + 1] * scale
        top = jnp.maximum(jnp.maximum(first, last), 0.0)
        first, mid, last = jnp.exp(first - top), jnp.exp(-top), jnp.exp(last - top)
        share = 1.0 / (first + mid + last)
        out[base] = first * share
        out[base + 1] = last * share
        out[base + 2] = total[base + 2] * scale
    out[6] = inverse


def edge_masked(first, last):
    column = lax.broadcasted_iota(jnp.int32, first.shape, 1)
    middle = 1.0 - first - last
    first = jnp.where(column == 0, 0.0, first)
    last = jnp.where(column == first.shape[1] - 1, 0.0, last)
    return first, middle, last


def column_of(row):
    n = row.shape[1]
    eye = lax.broadcasted_iota(jnp.int32, (n, n), 0) == lax.broadcasted_iota(jnp.int32, (n, n), 1)
    return jnp.sum(jnp.where(eye, jnp.broadcast_to(row, (n, n)), 0.0), axis=1, keepdims=True)


def rate_root(gate, bias):
    return lax.rsqrt(1.0 + jnp.exp(-(gate + bias)))


def blended(state, taps, h):
    left = pltpu.roll(state, 1, axis=2)
    right = pltpu.roll(state, state.shape[2] - 1, axis=2)
    a, b, c = (taps[k, pl.ds(h, 1), :] for k in range(3))
    return a * left + b * state + c * right


def row_at(step, upward, rows):
    return jnp.where(upward, rows - 1 - step, step)


def parity():
    return lax.axis_index("rows") & 1


def row_coefficients(feats, gates, inverse, gain, bias, h):
    values = feats[h].astype(jnp.float32)
    root = rate_root(gates[pl.ds(h, 1), :], bias)
    drive = root * (values * inverse[pl.ds(h, 1), :] * gain)
    shape = (values.shape[0] // 8, 8, values.shape[1])
    return (1.0 - root * root).reshape(shape), drive.reshape(shape)


def near_side(p0, p1, p2, p3, q0, q1, q2, q3, feats, gain, bias, near_taps, far_taps, far_gate, inverse, raw, decay, drive, kept, end):
    core, x = place()
    odd = parity()
    rows = feats.shape[0]
    near, far = odd * 3, 3 - odd * 3
    for other, pieces in ((0, (p0, p1, p2, p3)), (1, (q0, q1, q2, q3))):
        for s, piece in enumerate(pieces):
            at = lane_tile(core ^ other, x - s + 4)
            for k in range(3):
                raw[k, :, at] = piece[near + k]
            for k in range(2):
                far_taps[k, :, at] = piece[far + k]
            far_gate[:, at] = piece[far + 2]
            inverse[:, at] = piece[6]
    for k, tap in enumerate(edge_masked(raw[0], raw[1])):
        near_taps[k] = tap
    for k, tap in enumerate(edge_masked(far_taps[0], far_taps[1])):
        far_taps[k] = tap
    gain_column, bias_column = column_of(gain[...]), column_of(bias[...])
    gates = raw.at[2]

    def step(r, state):
        h = row_at(r, odd == 1, rows)
        d, q = row_coefficients(feats, gates, inverse, gain_column, bias_column, h)
        decay[h] = d
        drive[h] = q
        state = d * blended(state, near_taps, h) + q
        kept[h] = state
        return state

    end[...] = lax.fori_loop(0, rows, step, jnp.zeros(end.shape, jnp.float32))


def far_side(far_gate, inverse, feats, gain, bias, decay, drive):
    gain_column, bias_column = column_of(gain[...]), column_of(bias[...])

    def step(h, carry):
        decay[h], drive[h] = row_coefficients(feats, far_gate, inverse, gain_column, bias_column, h)
        return carry

    lax.fori_loop(0, feats.shape[0], step, 0)


def partner_side(raw, bias, taps, decay):
    bias_column = column_of(bias[...])
    for k, tap in enumerate(edge_masked(raw[0], raw[1])):
        taps[k] = tap

    def step(h, carry):
        root = rate_root(raw[2, pl.ds(h, 1), :], bias_column)
        decay[h] = (1.0 - root * root).reshape(decay.shape[1:])
        return carry

    lax.fori_loop(0, decay.shape[0], step, 0)


def scan_rows(state, upward, decay, drive, taps, emit):
    rows = decay.shape[0]

    def step(r, state):
        h = row_at(r, upward, rows)
        state = decay[h] * blended(state, taps, h)
        if drive is not None:
            state = state + drive[h]
        if emit is not None:
            emit(h, state)
        return state

    return lax.fori_loop(0, rows, step, state)


def turns(stage):
    position = lax.axis_index("rows")
    pair, odd = position >> 1, position & 1
    last = 3 - pair
    far = jnp.where(odd == 1, pair, last)
    return odd, far == stage, 3 - far == stage


def first_stage(partner_end, decay, drive, taps, kept_in, kept, leaving):
    odd, far, _ = turns(0)

    def emit(h, state):
        kept[h] = state

    @pl.when(far)
    def _():
        leaving[...] = scan_rows(partner_end[...], odd == 0, decay, drive, taps, emit)

    @pl.when(jnp.logical_not(far))
    def _():
        kept[...] = kept_in[...]


def later_stage(stage, final, *refs):
    if final:
        kept, refs = refs[0], refs[1:]
    far_in, near_in, partner_end, pd, pt, nd, nq, nt, fd, fq, ft = refs[:11]
    *before, out, leaving = refs[11:]
    odd, far, near = turns(stage)

    def emit(h, state):
        if final:
            out[h] = (kept[h] * state).reshape(out.shape[1:]).astype(out.dtype)
        else:
            out[h] = state

    @pl.when(far)
    def _():
        state = scan_rows(far_in[...], odd == 0, pd, None, pt, None) + partner_end[...]
        leaving[...] = scan_rows(state, odd == 0, fd, fq, ft, emit)

    @pl.when(near)
    def _():
        leaving[...] = scan_rows(near_in[...], odd == 1, nd, nq, nt, emit)

    if before:

        @pl.when(jnp.logical_not(far | near))
        def _():
            out[...] = before[0][...]


def chan_shift(value, target):
    return lax.ppermute(value, "chan", [(i, target(i)) for i in range(32)])


def along_x(value, s):
    return chan_shift(value, lambda i: (i & ~6) | ((((i >> 1) + s) & 3) << 1))


def along_y(value, s):
    return chan_shift(value, lambda i: (i & 7) | ((((i >> 3) + s) & 3) << 3))


def other_core(value):
    return chan_shift(value, lambda i: i ^ 1)


def shards(feats, norm_gain, proj_weight, chan_bias):
    rows, chans, cols = feats.shape
    gain, bias = norm_gain.reshape(1, chans), chan_bias.reshape(1, chans)
    piece = f32(SLOTS, rows, LANES)
    half = f32(4, SLOTS, rows, LANES)
    keep, send = pl.pallas_call(
        project,
        out_shape=(half, half),
        in_specs=[VMEM] * 3,
        out_specs=(VMEM, VMEM),
        scratch_shapes=[pltpu.VMEM((18 * rows, rows * chans), jnp.bfloat16)],
        compiler_params=pltpu.CompilerParams(vmem_limit_bytes=40 << 20),
    )(feats, gain, proj_weight)
    mine, *others = call(join_cores, (piece,) * 4, keep, other_core(send))
    part = call(join_x, piece, mine, *(along_x(v, s + 1) for s, v in enumerate(others)))
    whole = call(join_y, piece, part, *(along_y(part, s) for s in (1, 2, 3)))
    pieces = [whole] + [along_x(whole, s) for s in (1, 2, 3)]
    pieces = pieces + [other_core(v) for v in pieces]

    state = f32(chans // 8, 8, cols)
    block = f32(rows, chans // 8, 8, cols)
    taps = f32(3, rows, cols)
    line = f32(rows, cols)
    near_taps, far_taps, far_gate, inverse, raw, near_decay, near_drive, kept, end = call(
        near_side, (taps, taps, line, line, taps, block, block, block, state), *pieces, feats, gain, bias
    )

    def swapped(value):
        return lax.ppermute(value, "rows", [(p, p ^ 1) for p in range(8)])

    partner_end = swapped(end)
    partner_raw = swapped(raw)
    far_decay, far_drive = call(far_side, (block, block), far_gate, inverse, feats, gain, bias)
    kept, leaving = call(
        first_stage, (block, state), partner_end, far_decay, far_drive, far_taps, kept, aliases={4: 0}
    )
    partner_taps, partner_decay = call(partner_side, (taps, block), partner_raw, bias)
    shared = (
        partner_end, partner_decay, partner_taps, near_decay, near_drive, near_taps, far_decay, far_drive, far_taps,
    )
    out = None
    for stage in (1, 2, 3):
        t = stage - 1
        far_in = lax.ppermute(leaving, "rows", [(2 * t + 1, 2 * t + 3), (6 - 2 * t, 4 - 2 * t)])
        near_in = lax.ppermute(leaving, "rows", [(2 * t + 1, 2 * t + 2), (6 - 2 * t, 5 - 2 * t)])

        def kernel(*refs, stage=stage):
            later_stage(stage, stage > 1, *refs)

        args = (far_in, near_in, *shared)
        if stage == 1:
            kept, leaving = call(kernel, (block, state), *args, kept, aliases={11: 0})
        elif stage == 2:
            made = jax.ShapeDtypeStruct(feats.shape, jnp.bfloat16)
            out, leaving = call(kernel, (made, state), kept, *args)
        else:
            out, _ = call(kernel, (made, state), kept, *args, out, aliases={12: 0})
    return out


def solution(mesh):
    in_specs = (P("rows", "chan", None), P("chan"), P(None, "chan"), P("chan"))
    out_specs = P("rows", "chan", None)
    return jax.shard_map(shards, mesh=mesh, in_specs=in_specs, out_specs=out_specs, check_vma=False)
```

```python
import functools

import jax
import jax.numpy as jnp
from jax import lax
from jax.experimental import pallas as pl
from jax.experimental.pallas import tpu as pltpu
from jax.sharding import PartitionSpec as P

CHANNELS = 1024
EPSILON = 1e-05
LANES = 128
UNROLL = 16
SLOTS = 7

VMEM = pl.BlockSpec(memory_space=pltpu.VMEM)


def call(kernel, outs, *args, aliases=None, limit=40, name=None):
    return pl.pallas_call(
        kernel,
        out_shape=outs,
        in_specs=[VMEM] * len(args),
        out_specs=jax.tree.map(lambda _: VMEM, outs),
        input_output_aliases=aliases or {},
        compiler_params=pltpu.CompilerParams(vmem_limit_bytes=limit << 20),
        name=name,
    )(*args)


def f32(*shape):
    return jax.ShapeDtypeStruct(shape, jnp.float32)


def place():
    chan = lax.axis_index("chan")
    return chan & 1, (chan >> 1) & 3


def lane_tile(core, x):
    return pl.ds(pl.multiple_of((core * 4 + (x & 3)) * LANES, LANES), LANES)


def project(feats_in, gain_in, weight_in, keep, send, feats, gain, weight, wide, sems):
    core, x = place()
    rows, chans, _ = feats.shape
    order = [(half, s, lane_tile(core ^ half, x + s)) for half in (1, 0) for s in range(4)]
    sources = [(gain_in, gain), (weight_in, weight)]
    sources += [(feats_in.at[:, :, at], feats.at[:, :, at]) for _, _, at in order]
    copies = [pltpu.make_async_copy(a, b, sems.at[k]) for k, (a, b) in enumerate(sources)]
    for copy in copies:
        copy.start()
    copies[0].wait()
    copies[1].wait()
    w, g = weight[...], gain[...]
    picked = [w[0:1] - w[1:2], w[2:3] - w[1:2], w[6:7], w[3:4] - w[4:5], w[5:6] - w[4:5], w[7:8]]
    scaled = [p * g for p in picked]
    depth = rows * chans
    spot = lax.broadcasted_iota(jnp.int32, (chans, depth), 1) % chans
    picks = (spot == lax.broadcasted_iota(jnp.int32, (chans, depth), 0)).astype(jnp.bfloat16)
    band = lax.broadcasted_iota(jnp.int32, (rows, depth), 1) // chans
    own = band == lax.broadcasted_iota(jnp.int32, (rows, depth), 0)
    rest = jnp.concatenate(scaled + scaled[:2], axis=0)
    for part in range(3):
        head = rest.astype(jnp.bfloat16)
        rest = rest - head.astype(jnp.float32)
        spread_out = jnp.dot(head, picks, preferred_element_type=jnp.float32)
        for j in range(6):
            row = jnp.broadcast_to(spread_out[j : j + 1], (rows, depth))
            at = (part * 6 + j) * rows
            wide[at : at + rows] = jnp.where(own, row, 0.0).astype(jnp.bfloat16)
    for (half, s, at), copy in zip(order, copies[2:]):
        copy.wait()
        out = send if half else keep
        block = feats[:, :, at]
        sums = jnp.dot(wide[...], block.reshape(depth, LANES), preferred_element_type=jnp.float32)
        sums = sums[0 : 6 * rows] + sums[6 * rows : 12 * rows] + sums[12 * rows :]
        out[s, 0:6] = sums.reshape(6, rows, LANES)
        values = block.astype(jnp.float32)
        out[s, 6] = jnp.sum(values * values, axis=1)


def join_cores(keep, arrived, *outs):
    for s, out in enumerate(outs):
        out[...] = keep[s] + arrived[s]


def join_x(a, b, c, d, out):
    out[...] = (a[...] + b[...]) + (c[...] + d[...])


def join_y(a, b, c, d, out):
    total = [(a[j] + b[j]) + (c[j] + d[j]) for j in range(SLOTS)]
    inverse = lax.rsqrt(total[6] / CHANNELS + EPSILON)
    scale = inverse * CHANNELS**-0.5
    for base in (0, 3):
        first, last = total[base] * scale, total[base + 1] * scale
        top = jnp.maximum(jnp.maximum(first, last), 0.0)
        first, mid, last = jnp.exp(first - top), jnp.exp(-top), jnp.exp(last - top)
        share = 1.0 / (first + mid + last)
        out[base] = first * share
        out[base + 1] = last * share
        out[base + 2] = total[base + 2] * scale
    out[6] = inverse


def edge_masked(first, last):
    column = lax.broadcasted_iota(jnp.int32, first.shape, 1)
    middle = 1.0 - first - last
    first = jnp.where(column == 0, 0.0, first)
    last = jnp.where(column == first.shape[1] - 1, 0.0, last)
    return first, middle, last


def column_of(row):
    n = row.shape[1]
    eye = lax.broadcasted_iota(jnp.int32, (n, n), 0) == lax.broadcasted_iota(jnp.int32, (n, n), 1)
    return jnp.sum(jnp.where(eye, jnp.broadcast_to(row, (n, n)), 0.0), axis=1, keepdims=True)


def rate_root(gate, bias):
    return lax.rsqrt(1.0 + jnp.exp(-(gate + bias)))


def blended(state, taps, h):
    left = pltpu.roll(state, 1, axis=2)
    right = pltpu.roll(state, state.shape[2] - 1, axis=2)
    a, b, c = (taps[k, pl.ds(h, 1), :] for k in range(3))
    return a * left + b * state + c * right


def row_at(step, upward, rows):
    return jnp.where(upward, rows - 1 - step, step)


def parity():
    return lax.axis_index("rows") & 1


def row_coefficients(feats, gates, inverse, gain, bias, h):
    values = feats[h].astype(jnp.float32)
    root = rate_root(gates[pl.ds(h, 1), :], bias)
    drive = root * (values * inverse[pl.ds(h, 1), :] * gain)
    shape = (values.shape[0] // 8, 8, values.shape[1])
    return (1.0 - root * root).reshape(shape), drive.reshape(shape)


def near_side(p0, p1, p2, p3, q0, q1, q2, q3, feats, gain, bias, near_taps, far_taps, far_gate, inverse, raw, decay, drive, kept, end):
    core, x = place()
    odd = parity()
    rows = feats.shape[0]
    near, far = odd * 3, 3 - odd * 3
    for other, pieces in ((0, (p0, p1, p2, p3)), (1, (q0, q1, q2, q3))):
        for s, piece in enumerate(pieces):
            at = lane_tile(core ^ other, x - s + 4)
            for k in range(3):
                raw[k, :, at] = piece[near + k]
            for k in range(2):
                far_taps[k, :, at] = piece[far + k]
            far_gate[:, at] = piece[far + 2]
            inverse[:, at] = piece[6]
    for k, tap in enumerate(edge_masked(raw[0], raw[1])):
        near_taps[k] = tap
    for k, tap in enumerate(edge_masked(far_taps[0], far_taps[1])):
        far_taps[k] = tap
    gain_column, bias_column = column_of(gain[...]), column_of(bias[...])
    gates = raw.at[2]

    def step(r, state):
        h = row_at(r, odd == 1, rows)
        d, q = row_coefficients(feats, gates, inverse, gain_column, bias_column, h)
        decay[h] = d
        drive[h] = q
        state = d * blended(state, near_taps, h) + q
        kept[h] = state
        return state

    end[...] = lax.fori_loop(0, rows, step, jnp.zeros(end.shape, jnp.float32), unroll=2)


def far_side(far_gate, inverse, feats, gain, bias, decay, drive):
    gain_column, bias_column = column_of(gain[...]), column_of(bias[...])

    def step(h, carry):
        decay[h], drive[h] = row_coefficients(feats, far_gate, inverse, gain_column, bias_column, h)
        return carry

    lax.fori_loop(0, feats.shape[0], step, 0)


def partner_side(raw, bias, taps, decay):
    bias_column = column_of(bias[...])
    for k, tap in enumerate(edge_masked(raw[0], raw[1])):
        taps[k] = tap

    def step(h, carry):
        root = rate_root(raw[2, pl.ds(h, 1), :], bias_column)
        decay[h] = (1.0 - root * root).reshape(decay.shape[1:])
        return carry

    lax.fori_loop(0, decay.shape[0], step, 0)


def scan_rows(state, upward, decay, drive, taps, emit):
    rows = decay.shape[0]

    def step(r, state):
        h = row_at(r, upward, rows)
        state = decay[h] * blended(state, taps, h)
        if drive is not None:
            state = state + drive[h]
        if emit is not None:
            emit(h, state)
        return state

    return lax.fori_loop(0, rows, step, state, unroll=UNROLL)


def turn():
    position = lax.axis_index("rows")
    pair, odd = position >> 1, position & 1
    return odd, jnp.where(odd == 1, pair, 3 - pair)


def far_stage(stage, *refs):
    arrived, partner_end = refs[0], refs[1]
    if stage:
        pd, pt, refs = refs[2], refs[3], refs[4:]
    else:
        refs = refs[1:]
    if stage:
        fd, fq, ft, kept_in, leaving_in, kept, leaving = refs
    else:
        fd, fq, ft, kept_in, kept, leaving = refs[1:]
    odd, when = turn()

    def emit(h, state):
        kept[h] = state

    @pl.when(when == stage)
    def _():
        state = arrived[...]
        if stage:
            state = scan_rows(state, odd == 0, pd, None, pt, None) + partner_end[...]
        leaving[...] = scan_rows(state, odd == 0, fd, fq, ft, emit)

    @pl.when(when != stage)
    def _():
        kept[...] = kept_in[...]
        if stage:
            leaving[...] = leaving_in[...]


def last_stage(near_in, far_in, partner_end, pd, pt, fd, fq, ft, nd, nq, nt, kept, out, held, sems):
    odd, when = turn()
    rows = held.shape[0]

    def copy(h):
        return pltpu.make_async_copy(held.at[h], out.at[h], sems.at[h])

    def emit(h, state):
        held[h] = (kept[h] * state).reshape(held.shape[1:]).astype(held.dtype)
        copy(h).start()

    @pl.when(when == 3)
    def _():
        state = scan_rows(far_in[...], odd == 0, pd, None, pt, None) + partner_end[...]
        scan_rows(state, odd == 0, fd, fq, ft, emit)

    @pl.when(when != 3)
    def _():
        scan_rows(near_in[...], odd == 1, nd, nq, nt, emit)

    for h in range(rows):
        copy(h).wait()


def chan_shift(value, target):
    return lax.ppermute(value, "chan", [(i, target(i)) for i in range(32)])


def along_x(value, s):
    return chan_shift(value, lambda i: (i & ~6) | ((((i >> 1) + s) & 3) << 1))


def along_y(value, s):
    return chan_shift(value, lambda i: (i & 7) | ((((i >> 3) + s) & 3) << 3))


def other_core(value):
    return chan_shift(value, lambda i: i ^ 1)


def shards(feats, norm_gain, proj_weight, chan_bias):
    rows, chans, cols = feats.shape
    gain, bias = norm_gain.reshape(1, chans), chan_bias.reshape(1, chans)
    piece = f32(SLOTS, rows, LANES)
    half = f32(4, SLOTS, rows, LANES)
    keep, send = pl.pallas_call(
        project,
        out_shape=(half, half),
        in_specs=[pl.BlockSpec(memory_space=pltpu.HBM)] * 3,
        out_specs=(VMEM, VMEM),
        scratch_shapes=[
            pltpu.VMEM(feats.shape, feats.dtype),
            pltpu.VMEM(gain.shape, gain.dtype),
            pltpu.VMEM(proj_weight.shape, proj_weight.dtype),
            pltpu.VMEM((18 * rows, rows * chans), jnp.bfloat16),
            pltpu.SemaphoreType.DMA((10,)),
        ],
        compiler_params=pltpu.CompilerParams(vmem_limit_bytes=40 << 20),
    )(*(pltpu.with_memory_space_constraint(v, pltpu.HBM) for v in (feats, gain, proj_weight)))
    mine, *others = call(join_cores, (piece,) * 4, keep, other_core(send))
    part = call(join_x, piece, mine, *(along_x(v, s + 1) for s, v in enumerate(others)))
    whole = call(join_y, piece, part, *(along_y(part, s) for s in (1, 2, 3)))
    pieces = [whole] + [along_x(whole, s) for s in (1, 2, 3)]
    pieces = pieces + [other_core(v) for v in pieces]

    state = f32(chans // 8, 8, cols)
    block = f32(rows, chans // 8, 8, cols)
    taps = f32(3, rows, cols)
    line = f32(rows, cols)
    near_taps, far_taps, far_gate, inverse, raw, near_decay, near_drive, kept, end = call(
        near_side, (taps, taps, line, line, taps, block, block, block, state), *pieces, feats, gain, bias
    )

    def along_rows(value, pairs):
        return lax.ppermute(value, "rows", pairs)

    swap = [(p, p ^ 1) for p in range(8)]
    partner_end = along_rows(end, swap)
    far_decay, far_drive = call(far_side, (block, block), far_gate, inverse, feats, gain, bias)
    far = (far_decay, far_drive, far_taps)
    partner_raw = along_rows(raw, swap)
    kept, leaving = call(
        functools.partial(far_stage, 0), (block, state), partner_end, partner_end, *far, kept, aliases={5: 0}
    )
    partner_taps, partner_decay = call(partner_side, (taps, block), partner_raw, bias)
    partner = (partner_end, partner_decay, partner_taps)
    for stage in (1, 2):
        t = stage - 1
        arrived = along_rows(leaving, [(2 * t + 1, 2 * t + 3), (6 - 2 * t, 4 - 2 * t)])
        kept, leaving = call(
            functools.partial(far_stage, stage), (block, state), arrived, *partner, *far, kept, leaving,
            aliases={7: 0, 8: 1},
        )
    near_in = along_rows(leaving, [(1, 2), (2, 1), (3, 4), (4, 3), (5, 6), (6, 5)])
    far_in = along_rows(leaving, [(5, 7), (2, 0)])
    return pl.pallas_call(
        last_stage,
        out_shape=jax.ShapeDtypeStruct(feats.shape, jnp.bfloat16),
        in_specs=[VMEM] * 12,
        out_specs=pl.BlockSpec(memory_space=pl.ANY),
        scratch_shapes=[pltpu.VMEM(feats.shape, jnp.bfloat16), pltpu.SemaphoreType.DMA((rows,))],
        compiler_params=pltpu.CompilerParams(vmem_limit_bytes=40 << 20),
    )(near_in, far_in, *partner, *far, near_decay, near_drive, near_taps, kept)


def solution(mesh):
    in_specs = (P("rows", "chan", None), P("chan"), P(None, "chan"), P("chan"))
    out_specs = P("rows", "chan", None)
    return jax.shard_map(shards, mesh=mesh, in_specs=in_specs, out_specs=out_specs, check_vma=False)
```

```python
import functools

import jax
import jax.numpy as jnp
from jax import lax
from jax.experimental import pallas as pl
from jax.experimental.pallas import tpu as pltpu
from jax.sharding import PartitionSpec as P

CHANNELS = 1024
EPSILON = 1e-05
LANES = 128
TILES = 8
CHUNK = 8
SLOTS = 7

VMEM = pl.BlockSpec(memory_space=pltpu.VMEM)


def call(kernel, outs, *args, aliases=None, limit=24, name=None):
    return pl.pallas_call(
        kernel,
        out_shape=outs,
        in_specs=[VMEM] * len(args),
        out_specs=jax.tree.map(lambda _: VMEM, outs),
        input_output_aliases=aliases or {},
        compiler_params=pltpu.CompilerParams(vmem_limit_bytes=limit << 20),
        name=name,
    )(*args)


def f32(*shape):
    return jax.ShapeDtypeStruct(shape, jnp.float32)


def place():
    chan = lax.axis_index("chan")
    return chan & 1, (chan >> 1) & 3


def lane_tile(core, x):
    return pl.ds(pl.multiple_of((core * 4 + (x & 3)) * LANES, LANES), LANES)


def exchanged(tiles):
    size = LANES // TILES
    block = lax.broadcasted_iota(jnp.int32, tiles[0].shape, 1) // size
    tiles = list(tiles)
    for bit in range(3):
        step = 1 << bit
        upper = (block >> bit) & 1 == 1
        for m in range(TILES):
            if m & step:
                continue
            low, high = tiles[m], tiles[m + step]
            tiles[m] = jnp.where(upper, turned(high, size * step), low)
            tiles[m + step] = jnp.where(upper, high, turned(low, -size * step))
    return tiles


def shuffled(tiles, outer):
    lane = lax.broadcasted_iota(jnp.int32, tiles[0].shape, 1)
    source = (lane % outer) * (LANES // outer) + lane // outer
    return [jnp.take_along_axis(tile, source, axis=1) for tile in tiles]


def woven(tiles):
    return exchanged(shuffled(tiles, LANES // TILES))


def unwoven(tiles):
    return shuffled(exchanged(tiles), TILES)


def project(feats_in, gain_in, weight_in, bias_in, keep, send, feats, gain_column, bias_column, gain, weight, bias, wide, sums, sems):
    core, x = place()
    rows, chans, cols = feats.shape
    sources = [(gain_in, gain), (weight_in, weight), (bias_in, bias)]
    sources += [(feats_in.at[at], feats.at[at]) for at in (pl.ds(k, CHUNK) for k in range(0, rows, CHUNK))]
    copies = [pltpu.make_async_copy(a, b, sems.at[k]) for k, (a, b) in enumerate(sources)]
    for copy in copies:
        copy.start()
    for copy in copies[:3]:
        copy.wait()
    w, g = weight[...], gain[...]
    gain_column[...] = jnp.broadcast_to(column_of(g), gain_column.shape)
    bias_column[...] = jnp.broadcast_to(column_of(bias[...]), bias_column.shape)
    picked = [w[0:1] - w[1:2], w[2:3] - w[1:2], w[6:7], w[3:4] - w[4:5], w[5:6] - w[4:5], w[7:8]]
    scaled = [p * g for p in picked]
    depth = rows * chans
    spot = lax.broadcasted_iota(jnp.int32, (chans, depth), 1) % chans
    picks = (spot == lax.broadcasted_iota(jnp.int32, (chans, depth), 0)).astype(jnp.bfloat16)
    band = lax.broadcasted_iota(jnp.int32, (rows, depth), 1) // chans
    own = band == lax.broadcasted_iota(jnp.int32, (rows, depth), 0)
    rest = jnp.concatenate(scaled + scaled[:2], axis=0)
    for part in range(3):
        head = rest.astype(jnp.bfloat16)
        rest = rest - head.astype(jnp.float32)
        spread_out = jnp.dot(head, picks, preferred_element_type=jnp.float32)
        for j in range(6):
            row = jnp.broadcast_to(spread_out[j : j + 1], (rows, depth))
            at = (part * 6 + j) * rows
            wide[at : at + rows] = jnp.where(own, row, 0.0).astype(jnp.bfloat16)
    for copy in copies[3:]:
        copy.wait()
    for m in range(TILES):
        block = feats[:, :, m * LANES : (m + 1) * LANES]
        made = jnp.dot(wide[...], block.reshape(depth, LANES), preferred_element_type=jnp.float32)
        sums[m, 0 : 6 * rows] = made[0 : 6 * rows] + made[6 * rows : 12 * rows] + made[12 * rows :]
        values = block.astype(jnp.float32)
        sums[m, 6 * rows :] = jnp.sum(values * values, axis=1)
    tiles = woven([sums[m] for m in range(TILES)])
    for side in range(2):

        @pl.when(core == side)
        def _():
            for m, tile in enumerate(tiles):
                out = keep if m >> 2 == side else send
                out[((m & 3) - x) & 3] = tile.reshape(SLOTS, rows, LANES)


def weave_rows(first, feats, gain_column, gained):
    def step(h, carry):
        line = feats[first + h].astype(jnp.float32) * gain_column[:, :1]
        put(gained, h, [tile.reshape(-1, 8, LANES) for tile in woven(tiles_of(line))])
        return carry

    lax.fori_loop(0, gained.shape[0], step, 0, unroll=4)


def join_cores(keep, arrived, *outs):
    for s, out in enumerate(outs):
        out[...] = keep[s] + arrived[s]


def join_x(a, b, c, d, out):
    out[...] = (a[...] + b[...]) + (c[...] + d[...])


def join_y(a, b, c, d, out):
    total = [(a[j] + b[j]) + (c[j] + d[j]) for j in range(SLOTS)]
    inverse = lax.rsqrt(total[6] / CHANNELS + EPSILON)
    scale = inverse * CHANNELS**-0.5
    for base in (0, 3):
        first, last = total[base] * scale, total[base + 1] * scale
        top = jnp.maximum(jnp.maximum(first, last), 0.0)
        first, mid, last = jnp.exp(first - top), jnp.exp(-top), jnp.exp(last - top)
        share = 1.0 / (first + mid + last)
        out[base] = first * share
        out[base + 1] = last * share
        out[base + 2] = total[base + 2] * scale
    out[6] = inverse


def edge_masked(first, last):
    column = lax.broadcasted_iota(jnp.int32, first.shape, 1)
    middle = 1.0 - first - last
    first = jnp.where(column == 0, 0.0, first)
    last = jnp.where(column == first.shape[1] - 1, 0.0, last)
    return first, middle, last


def column_of(row):
    n = row.shape[1]
    eye = lax.broadcasted_iota(jnp.int32, (n, n), 0) == lax.broadcasted_iota(jnp.int32, (n, n), 1)
    return jnp.sum(jnp.where(eye, jnp.broadcast_to(row, (n, n)), 0.0), axis=1, keepdims=True)


def rate_root(gate, bias):
    return lax.rsqrt(1.0 + jnp.exp(-(gate + bias)))


def turned(tile, by):
    return pltpu.roll(tile, by % LANES, axis=tile.ndim - 1)


def tiles_of(line):
    return [line[..., m * LANES : (m + 1) * LANES] for m in range(TILES)]


def widen(ref, index, tiles):
    for m, tile in enumerate([turned(tiles[-1], 1), *tiles, turned(tiles[0], -1)]):
        ref[(*index, slice(m * LANES, (m + 1) * LANES))] = tile


def row_step(state, first, h, decay, drive, taps):
    after = []
    lines = [taps[j, pl.ds(h, 1), :] for j in range(3)]
    for k in range(1, len(state) - 1):
        m = first + k
        at = slice(m * LANES, (m + 1) * LANES)
        a, b, c = (line[:, at] for line in lines)
        value = decay[h, :, :, at] * (a * state[k - 1] + b * state[k] + c * state[k + 1])
        after.append(value if drive is None else value + drive[h, :, :, at])
    return after


def two_rows(state, h1, h2, decay, drive, taps):
    ends = [turned(state[-2], 1), turned(state[-1], 1)], [turned(state[0], -1), turned(state[1], -1)]
    middle = row_step(ends[0] + state + ends[1], -1, h1, decay, drive, taps)
    return middle[1:-1], row_step(middle, 0, h2, decay, drive, taps)


def put(ref, h, tiles):
    for m, tile in enumerate(tiles):
        ref[h, :, :, m * LANES : (m + 1) * LANES] = tile


def whole(tiles):
    return jnp.concatenate(tiles, axis=2)


def row_at(step, upward, rows):
    return jnp.where(upward, rows - 1 - step, step)


def parity():
    return lax.axis_index("rows") & 1


def row_coefficients(upper, lower, gates, inverse, bias, h, decay, drive):
    half = upper.shape[0]
    values = jnp.where(h < half, upper[h & (half - 1)], lower[h & (half - 1)])
    root = rate_root(gates[pl.ds(h, 1), :], bias)
    root = root.reshape(values.shape)
    force = root * (values * inverse[pl.ds(h, 1), :])
    every = slice(None)
    widen(decay, (h, every, every), tiles_of(1.0 - root * root))
    widen(drive, (h, every, every), tiles_of(force))


def put_taps(taps, first, last):
    for k, tap in enumerate(edge_masked(first, last)):
        widen(taps, (k, slice(None)), tiles_of(tap))


def near_side(p0, p1, p2, p3, q0, q1, q2, q3, upper, lower, bias, near_taps, far_taps, far_gate, inverse, raw, decay, drive, kept, end, far_raw):
    core, x = place()
    odd = parity()
    rows = raw.shape[1]
    near, far = odd * 3, 3 - odd * 3
    for other, pieces in ((0, (p0, p1, p2, p3)), (1, (q0, q1, q2, q3))):
        for s, piece in enumerate(pieces):
            at = lane_tile(core ^ other, x + s)
            for k in range(3):
                raw[k, :, at] = piece[near + k]
            for k in range(2):
                far_raw[k, :, at] = piece[far + k]
            far_gate[:, at] = piece[far + 2]
            inverse[:, at] = piece[6]
    put_taps(near_taps, raw[0], raw[1])
    put_taps(far_taps, far_raw[0], far_raw[1])
    bias_column = bias[:, :1]
    gates = raw.at[2]

    def step(r, state):
        h1, h2 = (row_at(2 * r + k, odd == 1, rows) for k in range(2))
        for h in (h1, h2):
            row_coefficients(upper, lower, gates, inverse, bias_column, h, decay, drive)
        middle, state = two_rows(state, h1, h2, decay, drive, near_taps)
        put(kept, h1, middle)
        put(kept, h2, state)
        return state

    state = tiles_of(jnp.zeros(end.shape, jnp.float32))
    end[...] = whole(lax.fori_loop(0, rows // 2, step, state, unroll=4))


def far_side(far_gate, inverse, upper, lower, bias, decay, drive):
    bias_column = bias[:, :1]

    def step(h, carry):
        row_coefficients(upper, lower, far_gate, inverse, bias_column, h, decay, drive)
        return carry

    lax.fori_loop(0, decay.shape[0], step, 0, unroll=4)


def partner_side(raw, bias, taps, decay):
    bias_column = bias[:, :1]
    put_taps(taps, raw[0], raw[1])
    every = slice(None)

    def step(h, carry):
        root = rate_root(raw[2, pl.ds(h, 1), :], bias_column)
        line = (1.0 - root * root).reshape(*decay.shape[1:3], raw.shape[2])
        widen(decay, (h, every, every), tiles_of(line))
        return carry

    lax.fori_loop(0, decay.shape[0], step, 0, unroll=4)


def scan_rows(state, upward, decay, drive, taps, emit):
    rows = decay.shape[0]

    def step(r, state):
        h1, h2 = (row_at(2 * r + k, upward, rows) for k in range(2))
        middle, state = two_rows(state, h1, h2, decay, drive, taps)
        if emit is not None:
            emit(h1, middle)
            emit(h2, state)
        return state

    return lax.fori_loop(0, rows // 2, step, state, unroll=rows // 2)


def carried_in(arrived, partner_end, odd, decay, taps):
    state = scan_rows(tiles_of(arrived[...]), odd == 0, decay, None, taps, None)
    return [a + b for a, b in zip(state, tiles_of(partner_end[...]))]


def turn():
    position = lax.axis_index("rows")
    pair, odd = position >> 1, position & 1
    return odd, jnp.where(odd == 1, pair, 3 - pair)


def far_stage(stage, *refs):
    arrived, partner_end = refs[0], refs[1]
    if stage:
        pd, pt, refs = refs[2], refs[3], refs[4:]
    else:
        refs = refs[1:]
    if stage:
        fd, fq, ft, kept_in, leaving_in, kept, leaving = refs
    else:
        fd, fq, ft, kept_in, kept, leaving = refs[1:]
    odd, when = turn()

    @pl.when(when == stage)
    def _():
        if stage:
            state = carried_in(arrived, partner_end, odd, pd, pt)
        else:
            state = tiles_of(arrived[...])
        leaving[...] = whole(scan_rows(state, odd == 0, fd, fq, ft, functools.partial(put, kept)))

    @pl.when(when != stage)
    def _():
        kept[...] = kept_in[...]
        if stage:
            leaving[...] = leaving_in[...]


def last_stage(near_in, far_in, partner_end, pd, pt, fd, fq, ft, nd, nq, nt, kept, out, mixed, made, sems):
    odd, when = turn()
    rows, chans, _ = made.shape

    def copy(h, k):
        return pltpu.make_async_copy(made.at[h], out.at[h], sems.at[k])

    def mix(h, tiles):
        for m, tile in enumerate(tiles):
            at = slice(m * LANES, (m + 1) * LANES)
            mixed[h, :, :, at] = kept[h, :, :, at] * tile

    def finish(h):
        tiles = [mixed[h, :, :, m * LANES : (m + 1) * LANES].reshape(chans, LANES) for m in range(TILES)]
        for m, tile in enumerate(unwoven(tiles)):
            made[h, :, m * LANES : (m + 1) * LANES] = tile.astype(made.dtype)
        copy(h, h).start()

    def scan_all(state, upward, decay, drive, taps):
        def pair(r):
            return [row_at(2 * r + k, upward, rows) for k in range(2)]

        def advance(r, state):
            middle, state = two_rows(state, *pair(r), decay, drive, taps)
            for h, tiles in zip(pair(r), (middle, state)):
                mix(h, tiles)
            return state

        def step(r, state):
            for h in pair(r - 1):
                finish(h)
            return advance(r, state)

        lax.fori_loop(1, rows // 2, step, advance(0, state))
        for h in pair(rows // 2 - 1):
            finish(h)

    @pl.when(when == 3)
    def _():
        scan_all(carried_in(far_in, partner_end, odd, pd, pt), odd == 0, fd, fq, ft)

    @pl.when(when != 3)
    def _():
        scan_all(tiles_of(near_in[...]), odd == 1, nd, nq, nt)

    for k in range(rows):
        copy(k, k).wait()


def chan_shift(value, target):
    return lax.ppermute(value, "chan", [(i, target(i)) for i in range(32)])


def along_x(value, s):
    return chan_shift(value, lambda i: (i & ~6) | ((((i >> 1) + s) & 3) << 1))


def along_y(value, s):
    return chan_shift(value, lambda i: (i & 7) | ((((i >> 3) + s) & 3) << 3))


def other_core(value):
    return chan_shift(value, lambda i: i ^ 1)


def shards(feats, norm_gain, proj_weight, chan_bias):
    rows, chans, cols = feats.shape
    gain, bias = norm_gain.reshape(1, chans), chan_bias.reshape(1, chans)
    piece = f32(SLOTS, rows, LANES)
    half = f32(4, SLOTS, rows, LANES)
    column = f32(chans, LANES)
    arguments = (feats, gain, proj_weight, bias)
    keep, send, feats, gain, bias = pl.pallas_call(
        project,
        out_shape=(half, half, jax.ShapeDtypeStruct(feats.shape, feats.dtype), column, column),
        in_specs=[pl.BlockSpec(memory_space=pltpu.HBM)] * 4,
        out_specs=(VMEM,) * 5,
        scratch_shapes=[
            pltpu.VMEM(gain.shape, gain.dtype),
            pltpu.VMEM(proj_weight.shape, proj_weight.dtype),
            pltpu.VMEM(bias.shape, bias.dtype),
            pltpu.VMEM((18 * rows, rows * chans), jnp.bfloat16),
            pltpu.VMEM((TILES, SLOTS * rows, LANES), jnp.float32),
            pltpu.SemaphoreType.DMA((3 + rows // CHUNK,)),
        ],
        compiler_params=pltpu.CompilerParams(vmem_limit_bytes=24 << 20),
    )(*(pltpu.with_memory_space_constraint(v, pltpu.HBM) for v in arguments))
    block = f32(rows, chans // 8, 8, cols)
    rows_half = f32(rows // 2, chans // 8, 8, cols)
    gained = [call(functools.partial(weave_rows, at), rows_half, feats, gain) for at in (0, rows // 2)]
    mine, *others = call(join_cores, (piece,) * 4, keep, other_core(send))
    part = call(join_x, piece, mine, *(along_x(v, s + 1) for s, v in enumerate(others)))
    part, gained[0] = lax.optimization_barrier((part, gained[0]))
    whole = call(join_y, piece, part, *(along_y(part, s) for s in (3, 2, 1)))
    whole, gained[1] = lax.optimization_barrier((whole, gained[1]))
    pieces = [whole] + [along_x(whole, s) for s in (3, 2, 1)]
    pieces = pieces + [other_core(v) for v in pieces]

    state = f32(chans // 8, 8, cols)
    wider = f32(rows, chans // 8, 8, cols + 2 * LANES)
    taps = f32(3, rows, cols + 2 * LANES)
    line, lines = f32(rows, cols), f32(3, rows, cols)
    near_taps, far_taps, far_gate, inverse, raw, near_decay, near_drive, kept, end = pl.pallas_call(
        near_side,
        out_shape=(taps, taps, line, line, lines, wider, wider, block, state),
        in_specs=[VMEM] * 11,
        out_specs=(VMEM,) * 9,
        scratch_shapes=[pltpu.VMEM((2, rows, cols), jnp.float32)],
        compiler_params=pltpu.CompilerParams(vmem_limit_bytes=24 << 20),
    )(*pieces, *gained, bias)

    def along_rows(value, pairs):
        return lax.ppermute(value, "rows", pairs)

    swap = [(p, p ^ 1) for p in range(8)]
    partner_end = along_rows(end, swap)
    far_decay, far_drive = call(far_side, (wider, wider), far_gate, inverse, *gained, bias)
    far = (far_decay, far_drive, far_taps)
    partner_raw = along_rows(raw, swap)
    kept, leaving = call(
        functools.partial(far_stage, 0), (block, state), partner_end, partner_end, *far, kept, aliases={5: 0}
    )
    partner_taps, partner_decay = call(partner_side, (taps, wider), partner_raw, bias)
    partner = (partner_end, partner_decay, partner_taps)
    for stage in (1, 2):
        t = stage - 1
        arrived = along_rows(leaving, [(2 * t + 1, 2 * t + 3), (6 - 2 * t, 4 - 2 * t)])
        kept, leaving = call(
            functools.partial(far_stage, stage), (block, state), arrived, *partner, *far, kept, leaving,
            aliases={7: 0, 8: 1},
        )
    near_in = along_rows(leaving, [(1, 2), (2, 1), (3, 4), (4, 3), (5, 6), (6, 5)])
    far_in = along_rows(leaving, [(5, 7), (2, 0)])
    return pl.pallas_call(
        last_stage,
        out_shape=jax.ShapeDtypeStruct(feats.shape, jnp.bfloat16),
        in_specs=[VMEM] * 12,
        out_specs=pl.BlockSpec(memory_space=pl.ANY),
        scratch_shapes=[
            pltpu.VMEM(block.shape, block.dtype),
            pltpu.VMEM(feats.shape, jnp.bfloat16),
            pltpu.SemaphoreType.DMA((rows,)),
        ],
        compiler_params=pltpu.CompilerParams(vmem_limit_bytes=24 << 20),
    )(near_in, far_in, *partner, *far, near_decay, near_drive, near_taps, kept)


def solution(mesh):
    in_specs = (P("rows", "chan", None), P("chan"), P(None, "chan"), P("chan"))
    out_specs = P("rows", "chan", None)
    return jax.shard_map(shards, mesh=mesh, in_specs=in_specs, out_specs=out_specs, check_vma=False)
```

```python
import functools

import jax
import jax.numpy as jnp
from jax import lax
from jax.experimental import pallas as pl
from jax.experimental.pallas import tpu as pltpu
from jax.sharding import PartitionSpec as P

CHANNELS = 1024
EPSILON = 1e-05
LANES = 128
TILES = 8
CHUNK = 8

FIRST_HOP = [(1, 3), (6, 4), (0, 1), (7, 6), (3, 2), (4, 5), (2, 0), (5, 7)]
SECOND_HOP = [(3, 5), (4, 2), (1, 3), (6, 4), (5, 6), (2, 1), (0, 7), (7, 0)]
THIRD_HOP = [(5, 7), (2, 0), (4, 5), (3, 2), (7, 6), (0, 1), (1, 3), (6, 4)]
LAST_PAIRS = [(1, 2), (2, 1), (3, 4), (4, 3), (5, 6), (6, 5), (0, 7), (7, 0)]
SLOTS = 7

VMEM = pl.BlockSpec(memory_space=pltpu.VMEM)


def call(kernel, outs, *args, aliases=None, limit=24, name=None):
    return pl.pallas_call(
        kernel,
        out_shape=outs,
        in_specs=[VMEM] * len(args),
        out_specs=jax.tree.map(lambda _: VMEM, outs),
        input_output_aliases=aliases or {},
        compiler_params=pltpu.CompilerParams(vmem_limit_bytes=limit << 20),
        name=name,
    )(*args)


def f32(*shape):
    return jax.ShapeDtypeStruct(shape, jnp.float32)


def place():
    chan = lax.axis_index("chan")
    return chan & 1, (chan >> 1) & 3


def lane_tile(core, x):
    return pl.ds(pl.multiple_of((core * 4 + (x & 3)) * LANES, LANES), LANES)


def turned(tile, by):
    return pltpu.roll(tile, by % LANES, axis=tile.ndim - 1)


def lane_of(tile):
    return lax.broadcasted_iota(jnp.int32, tile.shape, tile.ndim - 1)


def neighbour(tile, by):
    lane = lane_of(tile)
    wraps = lane < TILES if by > 0 else lane >= LANES - TILES
    return jnp.where(wraps, turned(tile, by * (TILES + 1)), turned(tile, by * TILES))


def exchanged(tiles):
    lane = lane_of(tiles[0])
    tiles = list(tiles)
    for bit in range(3):
        step = 1 << bit
        upper = (lane >> bit) & 1 == 1
        for m in range(TILES):
            if m & step:
                continue
            low, high = tiles[m], tiles[m + step]
            tiles[m] = jnp.where(upper, turned(high, step), low)
            tiles[m + step] = jnp.where(upper, high, turned(low, -step))
    return tiles


def project(feats_in, gain_in, weight_in, bias_in, keep, send, feats, gain_column, bias_column, gain, weight, bias, wide, sums, sems):
    core, x = place()
    rows, chans, cols = feats.shape
    sources = [(gain_in, gain), (weight_in, weight), (bias_in, bias)]
    sources += [(feats_in.at[at], feats.at[at]) for at in (pl.ds(k, CHUNK) for k in range(0, rows, CHUNK))]
    copies = [pltpu.make_async_copy(a, b, sems.at[k]) for k, (a, b) in enumerate(sources)]
    for copy in copies:
        copy.start()
    for copy in copies[:3]:
        copy.wait()
    w, g = weight[...], gain[...]
    gain_column[...] = jnp.broadcast_to(column_of(g), gain_column.shape)
    bias_column[...] = jnp.broadcast_to(column_of(bias[...]), bias_column.shape)
    picked = [w[0:1] - w[1:2], w[2:3] - w[1:2], w[6:7], w[3:4] - w[4:5], w[5:6] - w[4:5], w[7:8]]
    scaled = [p * g for p in picked]
    depth = rows * chans
    spot = lax.broadcasted_iota(jnp.int32, (chans, depth), 1) % chans
    picks = (spot == lax.broadcasted_iota(jnp.int32, (chans, depth), 0)).astype(jnp.bfloat16)
    band = lax.broadcasted_iota(jnp.int32, (rows, depth), 1) // chans
    own = band == lax.broadcasted_iota(jnp.int32, (rows, depth), 0)
    rest = jnp.concatenate(scaled + scaled[:2], axis=0)
    for part in range(3):
        head = rest.astype(jnp.bfloat16)
        rest = rest - head.astype(jnp.float32)
        spread_out = jnp.dot(head, picks, preferred_element_type=jnp.float32)
        for j in range(6):
            row = jnp.broadcast_to(spread_out[j : j + 1], (rows, depth))
            at = (part * 6 + j) * rows
            wide[at : at + rows] = jnp.where(own, row, 0.0).astype(jnp.bfloat16)
    for copy in copies[3:]:
        copy.wait()
    for m in range(TILES):
        block = feats[:, :, m * LANES : (m + 1) * LANES]
        made = jnp.dot(wide[...], block.reshape(depth, LANES), preferred_element_type=jnp.float32)
        sums[m, 0 : 6 * rows] = made[0 : 6 * rows] + made[6 * rows : 12 * rows] + made[12 * rows :]
        values = block.astype(jnp.float32)
        sums[m, 6 * rows :] = jnp.sum(values * values, axis=1)
    tiles = exchanged([sums[m] for m in range(TILES)])
    for side in range(2):

        @pl.when(core == side)
        def _():
            for m, tile in enumerate(tiles):
                out = keep if m >> 2 == side else send
                out[((m & 3) - x) & 3] = tile.reshape(SLOTS, rows, LANES)


def weave_rows(first, feats, gain_column, gained):
    def step(h, carry):
        tiles = exchanged(tiles_of(feats[first + h]))
        tiles = [tile.astype(jnp.float32) * gain_column[:, :1] for tile in tiles]
        put(gained, h, [tile.reshape(-1, 8, LANES) for tile in tiles])
        return carry

    lax.fori_loop(0, gained.shape[0], step, 0, unroll=4)


def join_cores(keep, arrived, *outs):
    for s, out in enumerate(outs):
        out[...] = keep[s] + arrived[s]


def join_x(a, b, c, d, out):
    out[...] = (a[...] + b[...]) + (c[...] + d[...])


def join_y(a, b, c, d, out):
    total = [(a[j] + b[j]) + (c[j] + d[j]) for j in range(SLOTS)]
    inverse = lax.rsqrt(total[6] / CHANNELS + EPSILON)
    scale = inverse * CHANNELS**-0.5
    for base in (0, 3):
        first, last = total[base] * scale, total[base + 1] * scale
        top = jnp.maximum(jnp.maximum(first, last), 0.0)
        first, mid, last = jnp.exp(first - top), jnp.exp(-top), jnp.exp(last - top)
        share = 1.0 / (first + mid + last)
        out[base] = first * share
        out[base + 1] = last * share
        out[base + 2] = total[base + 2] * scale
    out[6] = inverse


def edge_masked(first, last):
    column = lax.broadcasted_iota(jnp.int32, first.shape, 1)
    middle = 1.0 - first - last
    first = jnp.where(column == 0, 0.0, first)
    last = jnp.where(column == first.shape[1] - 1, 0.0, last)
    return first, middle, last


def column_of(row):
    n = row.shape[1]
    eye = lax.broadcasted_iota(jnp.int32, (n, n), 0) == lax.broadcasted_iota(jnp.int32, (n, n), 1)
    return jnp.sum(jnp.where(eye, jnp.broadcast_to(row, (n, n)), 0.0), axis=1, keepdims=True)


def rate_root(gate, bias):
    return lax.rsqrt(1.0 + jnp.exp(-(gate + bias)))


def tiles_of(line):
    return [line[..., m * LANES : (m + 1) * LANES] for m in range(TILES)]


def widen(ref, index, tiles):
    for m, tile in enumerate([neighbour(tiles[-1], 1), *tiles, neighbour(tiles[0], -1)]):
        ref[(*index, slice(m * LANES, (m + 1) * LANES))] = tile


def row_step(state, first, h, decay, drive, taps):
    after = []
    lines = [taps[j, pl.ds(h, 1), :] for j in range(3)]
    for k in range(1, len(state) - 1):
        m = first + k
        at = slice(m * LANES, (m + 1) * LANES)
        a, b, c = (line[:, at] for line in lines)
        value = decay[h, :, :, at] * (a * state[k - 1] + b * state[k] + c * state[k + 1])
        after.append(value if drive is None else value + drive[h, :, :, at])
    return after


def two_rows(state, h1, h2, decay, drive, taps):
    ends = [neighbour(tile, 1) for tile in state[-2:]], [neighbour(tile, -1) for tile in state[:2]]
    middle = row_step(ends[0] + state + ends[1], -1, h1, decay, drive, taps)
    return middle[1:-1], row_step(middle, 0, h2, decay, drive, taps)


def put(ref, h, tiles):
    for m, tile in enumerate(tiles):
        ref[h, :, :, m * LANES : (m + 1) * LANES] = tile


def whole(tiles):
    return jnp.concatenate(tiles, axis=2)


def row_at(step, upward, rows):
    return jnp.where(upward, rows - 1 - step, step)


def parity():
    return lax.axis_index("rows") & 1


def row_coefficients(upper, lower, gates, inverse, bias, h, decay, drive):
    half = upper.shape[0]
    values = jnp.where(h < half, upper[h & (half - 1)], lower[h & (half - 1)])
    root = rate_root(gates[pl.ds(h, 1), :], bias)
    root = root.reshape(values.shape)
    force = root * (values * inverse[pl.ds(h, 1), :])
    every = slice(None)
    widen(decay, (h, every, every), tiles_of(1.0 - root * root))
    widen(drive, (h, every, every), tiles_of(force))


def put_taps(taps, first, last):
    for k, tap in enumerate(edge_masked(first, last)):
        widen(taps, (k, slice(None)), tiles_of(tap))


def near_side(p0, p1, p2, p3, q0, q1, q2, q3, upper, lower, bias, near_taps, far_taps, far_gate, inverse, raw, decay, drive, kept, end, far_raw):
    core, x = place()
    odd = parity()
    rows = raw.shape[1]
    near, far = odd * 3, 3 - odd * 3
    for other, pieces in ((0, (p0, p1, p2, p3)), (1, (q0, q1, q2, q3))):
        for s, piece in enumerate(pieces):
            at = lane_tile(core ^ other, x + s)
            for k in range(3):
                raw[k, :, at] = piece[near + k]
            for k in range(2):
                far_raw[k, :, at] = piece[far + k]
            far_gate[:, at] = piece[far + 2]
            inverse[:, at] = piece[6]
    put_taps(near_taps, raw[0], raw[1])
    put_taps(far_taps, far_raw[0], far_raw[1])
    bias_column = bias[:, :1]
    gates = raw.at[2]

    def step(r, state):
        h1, h2 = (row_at(2 * r + k, odd == 1, rows) for k in range(2))
        for h in (h1, h2):
            row_coefficients(upper, lower, gates, inverse, bias_column, h, decay, drive)
        middle, state = two_rows(state, h1, h2, decay, drive, near_taps)
        put(kept, h1, middle)
        put(kept, h2, state)
        return state

    state = tiles_of(jnp.zeros(end.shape, jnp.float32))
    end[...] = whole(lax.fori_loop(0, rows // 2, step, state, unroll=4))


def far_side(far_gate, inverse, upper, lower, bias, decay, drive):
    bias_column = bias[:, :1]

    def step(h, carry):
        row_coefficients(upper, lower, far_gate, inverse, bias_column, h, decay, drive)
        return carry

    lax.fori_loop(0, decay.shape[0], step, 0, unroll=4)


def partner_side(raw, bias, taps, decay):
    bias_column = bias[:, :1]
    put_taps(taps, raw[0], raw[1])
    every = slice(None)

    def step(h, carry):
        root = rate_root(raw[2, pl.ds(h, 1), :], bias_column)
        line = (1.0 - root * root).reshape(*decay.shape[1:3], raw.shape[2])
        widen(decay, (h, every, every), tiles_of(line))
        return carry

    lax.fori_loop(0, decay.shape[0], step, 0, unroll=4)


def scan_rows(state, upward, decay, drive, taps, emit):
    rows = decay.shape[0]

    def step(r, state):
        h1, h2 = (row_at(2 * r + k, upward, rows) for k in range(2))
        middle, state = two_rows(state, h1, h2, decay, drive, taps)
        if emit is not None:
            emit(h1, middle)
            emit(h2, state)
        return state

    return lax.fori_loop(0, rows // 2, step, state, unroll=rows // 2)


def carried_in(arrived, partner_end, odd, decay, taps):
    state = scan_rows(tiles_of(arrived[...]), odd == 0, decay, None, taps, None)
    return [a + b for a, b in zip(state, tiles_of(partner_end[...]))]


def turn():
    position = lax.axis_index("rows")
    pair, odd = position >> 1, position & 1
    return odd, jnp.where(odd == 1, pair, 3 - pair)


def far_stage(stage, *refs):
    arrived, partner_end = refs[0], refs[1]
    if stage:
        pd, pt, refs = refs[2], refs[3], refs[4:]
    else:
        refs = refs[1:]
    if stage:
        fd, fq, ft, kept_in, leaving_in, kept, leaving = refs
    else:
        fd, fq, ft, kept_in, kept, leaving = refs[1:]
    odd, when = turn()

    @pl.when(when == stage)
    def _():
        if stage:
            state = carried_in(arrived, partner_end, odd, pd, pt)
        else:
            state = tiles_of(arrived[...])
        leaving[...] = whole(scan_rows(state, odd == 0, fd, fq, ft, functools.partial(put, kept)))

    @pl.when(when != stage)
    def _():
        kept[...] = kept_in[...]
        if stage:
            leaving[...] = leaving_in[...]


def last_stage(near_in, far_in, partner_end, pd, pt, fd, fq, ft, nd, nq, nt, kept, out, mixed, made, sems):
    odd, when = turn()
    rows, chans, _ = made.shape

    def copy(h, k):
        return pltpu.make_async_copy(made.at[h], out.at[h], sems.at[k])

    def mix(h, tiles):
        for m, tile in enumerate(tiles):
            at = slice(m * LANES, (m + 1) * LANES)
            mixed[h, :, at] = (kept[h, :, :, at] * tile).reshape(chans, LANES).astype(mixed.dtype)

    def finish(h):
        for m, tile in enumerate(exchanged(tiles_of(mixed[h]))):
            made[h, :, m * LANES : (m + 1) * LANES] = tile
        copy(h, h).start()

    def scan_all(state, upward, decay, drive, taps):
        def pair(r):
            return [row_at(2 * r + k, upward, rows) for k in range(2)]

        def advance(r, state):
            middle, state = two_rows(state, *pair(r), decay, drive, taps)
            for h, tiles in zip(pair(r), (middle, state)):
                mix(h, tiles)
            return state

        def step(r, state):
            for h in pair(r - 1):
                finish(h)
            return advance(r, state)

        lax.fori_loop(1, rows // 2, step, advance(0, state))
        for h in pair(rows // 2 - 1):
            finish(h)

    @pl.when(when == 3)
    def _():
        scan_all(carried_in(far_in, partner_end, odd, pd, pt), odd == 0, fd, fq, ft)

    @pl.when(when != 3)
    def _():
        scan_all(tiles_of(near_in[...]), odd == 1, nd, nq, nt)

    for k in range(rows):
        copy(k, k).wait()


def chan_shift(value, target):
    return lax.ppermute(value, "chan", [(i, target(i)) for i in range(32)])


def along_x(value, s):
    return chan_shift(value, lambda i: (i & ~6) | ((((i >> 1) + s) & 3) << 1))


def along_y(value, s):
    return chan_shift(value, lambda i: (i & 7) | ((((i >> 3) + s) & 3) << 3))


def other_core(value):
    return chan_shift(value, lambda i: i ^ 1)


def shards(feats, norm_gain, proj_weight, chan_bias):
    rows, chans, cols = feats.shape
    gain, bias = norm_gain.reshape(1, chans), chan_bias.reshape(1, chans)
    piece = f32(SLOTS, rows, LANES)
    half = f32(4, SLOTS, rows, LANES)
    column = f32(chans, LANES)
    arguments = (feats, gain, proj_weight, bias)
    keep, send, feats, gain, bias = pl.pallas_call(
        project,
        out_shape=(half, half, jax.ShapeDtypeStruct(feats.shape, feats.dtype), column, column),
        in_specs=[pl.BlockSpec(memory_space=pltpu.HBM)] * 4,
        out_specs=(VMEM,) * 5,
        scratch_shapes=[
            pltpu.VMEM(gain.shape, gain.dtype),
            pltpu.VMEM(proj_weight.shape, proj_weight.dtype),
            pltpu.VMEM(bias.shape, bias.dtype),
            pltpu.VMEM((18 * rows, rows * chans), jnp.bfloat16),
            pltpu.VMEM((TILES, SLOTS * rows, LANES), jnp.float32),
            pltpu.SemaphoreType.DMA((3 + rows // CHUNK,)),
        ],
        compiler_params=pltpu.CompilerParams(vmem_limit_bytes=24 << 20),
    )(*(pltpu.with_memory_space_constraint(v, pltpu.HBM) for v in arguments))
    block = f32(rows, chans // 8, 8, cols)
    rows_half = f32(rows // 2, chans // 8, 8, cols)
    gained = [call(functools.partial(weave_rows, at), rows_half, feats, gain) for at in (0, rows // 2)]
    mine, *others = call(join_cores, (piece,) * 4, keep, other_core(send))
    part = call(join_x, piece, mine, *(along_x(v, s + 1) for s, v in enumerate(others)))
    part, gained[0] = lax.optimization_barrier((part, gained[0]))
    whole = call(join_y, piece, part, *(along_y(part, s) for s in (3, 2, 1)))
    whole, gained[1] = lax.optimization_barrier((whole, gained[1]))
    pieces = [whole] + [along_x(whole, s) for s in (3, 2, 1)]
    pieces = pieces + [other_core(v) for v in pieces]

    state = f32(chans // 8, 8, cols)
    wider = f32(rows, chans // 8, 8, cols + 2 * LANES)
    taps = f32(3, rows, cols + 2 * LANES)
    line, lines = f32(rows, cols), f32(3, rows, cols)
    near_taps, far_taps, far_gate, inverse, raw, near_decay, near_drive, kept, end = pl.pallas_call(
        near_side,
        out_shape=(taps, taps, line, line, lines, wider, wider, block, state),
        in_specs=[VMEM] * 11,
        out_specs=(VMEM,) * 9,
        scratch_shapes=[pltpu.VMEM((2, rows, cols), jnp.float32)],
        compiler_params=pltpu.CompilerParams(vmem_limit_bytes=24 << 20),
    )(*pieces, *gained, bias)

    def along_rows(value, pairs):
        return lax.ppermute(value, "rows", pairs)

    swap = [(p, p ^ 1) for p in range(8)]
    partner_end = along_rows(end, swap)
    far_decay, far_drive = call(far_side, (wider, wider), far_gate, inverse, *gained, bias)
    far = (far_decay, far_drive, far_taps)
    partner_raw = along_rows(raw, swap)
    kept, leaving = call(
        functools.partial(far_stage, 0), (block, state), partner_end, partner_end, *far, kept, aliases={5: 0}
    )
    partner_taps, partner_decay = call(partner_side, (taps, wider), partner_raw, bias)
    partner = (partner_end, partner_decay, partner_taps)
    for stage, pairs in ((1, FIRST_HOP), (2, SECOND_HOP)):
        arrived = along_rows(leaving, pairs)
        kept, leaving = call(
            functools.partial(far_stage, stage), (block, state), arrived, *partner, *far, kept, leaving,
            aliases={7: 0, 8: 1},
        )
    near_in = along_rows(leaving, LAST_PAIRS)
    far_in = along_rows(leaving, THIRD_HOP)
    return pl.pallas_call(
        last_stage,
        out_shape=jax.ShapeDtypeStruct(feats.shape, jnp.bfloat16),
        in_specs=[VMEM] * 12,
        out_specs=pl.BlockSpec(memory_space=pl.ANY),
        scratch_shapes=[
            pltpu.VMEM(feats.shape, jnp.bfloat16),
            pltpu.VMEM(feats.shape, jnp.bfloat16),
            pltpu.SemaphoreType.DMA((rows,)),
        ],
        compiler_params=pltpu.CompilerParams(vmem_limit_bytes=24 << 20),
    )(near_in, far_in, *partner, *far, near_decay, near_drive, near_taps, kept)


def solution(mesh):
    in_specs = (P("rows", "chan", None), P("chan"), P(None, "chan"), P("chan"))
    out_specs = P("rows", "chan", None)
    return jax.shard_map(shards, mesh=mesh, in_specs=in_specs, out_specs=out_specs, check_vma=False)
```

```python
import functools

import jax
import jax.numpy as jnp
from jax import lax
from jax.experimental import pallas as pl
from jax.experimental.pallas import tpu as pltpu
from jax.sharding import PartitionSpec as P

CHANNELS = 1024
EPSILON = 1e-05
LANES = 128
TILES = 8
CHUNK = 8

FIRST_HOP = [(1, 3), (6, 4), (0, 1), (7, 6), (3, 2), (4, 5), (2, 0), (5, 7)]
SECOND_HOP = [(3, 5), (4, 2), (1, 3), (6, 4), (5, 6), (2, 1), (0, 7), (7, 0)]
THIRD_HOP = [(5, 7), (2, 0), (4, 5), (3, 2), (7, 6), (0, 1), (1, 3), (6, 4)]
LAST_PAIRS = [(1, 2), (2, 1), (3, 4), (4, 3), (5, 6), (6, 5), (0, 7), (7, 0)]
SLOTS = 7

VMEM = pl.BlockSpec(memory_space=pltpu.VMEM)


def call(kernel, outs, *args, aliases=None, limit=24, name=None):
    return pl.pallas_call(
        kernel,
        out_shape=outs,
        in_specs=[VMEM] * len(args),
        out_specs=jax.tree.map(lambda _: VMEM, outs),
        input_output_aliases=aliases or {},
        compiler_params=pltpu.CompilerParams(vmem_limit_bytes=limit << 20),
        name=name,
    )(*args)


def f32(*shape):
    return jax.ShapeDtypeStruct(shape, jnp.float32)


def place():
    chan = lax.axis_index("chan")
    return chan & 1, (chan >> 1) & 3


def lane_tile(core, x):
    return pl.ds(pl.multiple_of((core * 4 + (x & 3)) * LANES, LANES), LANES)


def turned(tile, by):
    return pltpu.roll(tile, by % LANES, axis=tile.ndim - 1)


def lane_of(tile):
    return lax.broadcasted_iota(jnp.int32, tile.shape, tile.ndim - 1)


def neighbour(tile, by):
    lane = lane_of(tile)
    wraps = lane < TILES if by > 0 else lane >= LANES - TILES
    return jnp.where(wraps, turned(tile, by * (TILES + 1)), turned(tile, by * TILES))


def exchanged(tiles):
    lane = lane_of(tiles[0])
    tiles = list(tiles)
    for bit in range(3):
        step = 1 << bit
        upper = (lane >> bit) & 1 == 1
        for m in range(TILES):
            if m & step:
                continue
            low, high = tiles[m], tiles[m + step]
            tiles[m] = jnp.where(upper, turned(high, step), low)
            tiles[m + step] = jnp.where(upper, high, turned(low, -step))
    return tiles


def project(feats_in, gain_in, weight_in, bias_in, keep, send, feats, gain_column, bias_column, gain, weight, bias, wide, sums, sems):
    core, x = place()
    rows, chans, cols = feats.shape
    sources = [(gain_in, gain), (weight_in, weight), (bias_in, bias)]
    sources += [(feats_in.at[at], feats.at[at]) for at in (pl.ds(k, CHUNK) for k in range(0, rows, CHUNK))]
    copies = [pltpu.make_async_copy(a, b, sems.at[k]) for k, (a, b) in enumerate(sources)]
    for copy in copies:
        copy.start()
    for copy in copies[:3]:
        copy.wait()
    w, g = weight[...], gain[...]
    gain_column[...] = jnp.broadcast_to(column_of(g), gain_column.shape)
    bias_column[...] = jnp.broadcast_to(column_of(bias[...]), bias_column.shape)
    picked = [w[0:1] - w[1:2], w[2:3] - w[1:2], w[6:7], w[3:4] - w[4:5], w[5:6] - w[4:5], w[7:8]]
    scaled = [p * g for p in picked]
    depth = rows * chans
    spot = lax.broadcasted_iota(jnp.int32, (chans, depth), 1) % chans
    picks = (spot == lax.broadcasted_iota(jnp.int32, (chans, depth), 0)).astype(jnp.bfloat16)
    band = lax.broadcasted_iota(jnp.int32, (rows, depth), 1) // chans
    own = band == lax.broadcasted_iota(jnp.int32, (rows, depth), 0)
    rest = jnp.concatenate(scaled + scaled[:2], axis=0)
    for part in range(3):
        head = rest.astype(jnp.bfloat16)
        rest = rest - head.astype(jnp.float32)
        spread_out = jnp.dot(head, picks, preferred_element_type=jnp.float32)
        for j in range(6):
            row = jnp.broadcast_to(spread_out[j : j + 1], (rows, depth))
            at = (part * 6 + j) * rows
            wide[at : at + rows] = jnp.where(own, row, 0.0).astype(jnp.bfloat16)
    for copy in copies[3:]:
        copy.wait()
    for m in range(TILES):
        block = feats[:, :, m * LANES : (m + 1) * LANES]
        made = jnp.dot(wide[...], block.reshape(depth, LANES), preferred_element_type=jnp.float32)
        sums[m, 0 : 6 * rows] = made[0 : 6 * rows] + made[6 * rows : 12 * rows] + made[12 * rows :]
        values = block.astype(jnp.float32)
        sums[m, 6 * rows :] = jnp.sum(values * values, axis=1)
    tiles = exchanged([sums[m] for m in range(TILES)])
    for side in range(2):

        @pl.when(core == side)
        def _():
            for m, tile in enumerate(tiles):
                out = keep if m >> 2 == side else send
                out[((m & 3) - x) & 3] = tile.reshape(SLOTS, rows, LANES)


def weave_rows(first, feats, gain_column, gained):
    def step(h, carry):
        tiles = exchanged(tiles_of(feats[first + h]))
        tiles = [tile.astype(jnp.float32) * gain_column[:, :1] for tile in tiles]
        put(gained, h, [tile.reshape(-1, 8, LANES) for tile in tiles])
        return carry

    lax.fori_loop(0, gained.shape[0], step, 0, unroll=4)


def join_cores(keep, arrived, *outs):
    for s, out in enumerate(outs):
        out[...] = keep[s] + arrived[s]


def join_x(a, b, c, d, out):
    out[...] = (a[...] + b[...]) + (c[...] + d[...])


def join_y(a, b, c, d, out):
    total = [(a[j] + b[j]) + (c[j] + d[j]) for j in range(SLOTS)]
    inverse = lax.rsqrt(total[6] / CHANNELS + EPSILON)
    scale = inverse * CHANNELS**-0.5
    for base in (0, 3):
        first, last = total[base] * scale, total[base + 1] * scale
        top = jnp.maximum(jnp.maximum(first, last), 0.0)
        first, mid, last = jnp.exp(first - top), jnp.exp(-top), jnp.exp(last - top)
        share = 1.0 / (first + mid + last)
        out[base] = first * share
        out[base + 1] = last * share
        out[base + 2] = total[base + 2] * scale
    out[6] = inverse


def edge_masked(first, last):
    column = lax.broadcasted_iota(jnp.int32, first.shape, 1)
    middle = 1.0 - first - last
    first = jnp.where(column == 0, 0.0, first)
    last = jnp.where(column == first.shape[1] - 1, 0.0, last)
    return first, middle, last


def column_of(row):
    n = row.shape[1]
    eye = lax.broadcasted_iota(jnp.int32, (n, n), 0) == lax.broadcasted_iota(jnp.int32, (n, n), 1)
    return jnp.sum(jnp.where(eye, jnp.broadcast_to(row, (n, n)), 0.0), axis=1, keepdims=True)


def rate_root(gate, bias):
    return lax.rsqrt(1.0 + jnp.exp(-(gate + bias)))


def tiles_of(line):
    return [line[..., m * LANES : (m + 1) * LANES] for m in range(TILES)]


def widen(ref, index, tiles):
    for m, tile in enumerate([neighbour(tiles[-1], 1), *tiles, neighbour(tiles[0], -1)]):
        ref[(*index, slice(m * LANES, (m + 1) * LANES))] = tile


def row_step(state, first, h, decay, drive, taps):
    after = []
    lines = [taps[j, pl.ds(h, 1), :] for j in range(3)]
    for k in range(1, len(state) - 1):
        m = first + k
        at = slice(m * LANES, (m + 1) * LANES)
        a, b, c = (line[:, at] for line in lines)
        value = decay[h, :, :, at] * (a * state[k - 1] + b * state[k] + c * state[k + 1])
        after.append(value if drive is None else value + drive[h, :, :, at])
    return after


def two_rows(state, h1, h2, decay, drive, taps):
    ends = [neighbour(tile, 1) for tile in state[-2:]], [neighbour(tile, -1) for tile in state[:2]]
    middle = row_step(ends[0] + state + ends[1], -1, h1, decay, drive, taps)
    return middle[1:-1], row_step(middle, 0, h2, decay, drive, taps)


def put(ref, h, tiles):
    for m, tile in enumerate(tiles):
        ref[h, :, :, m * LANES : (m + 1) * LANES] = tile


def whole(tiles):
    return jnp.concatenate(tiles, axis=2)


def row_at(step, upward, rows):
    return jnp.where(upward, rows - 1 - step, step)


def parity():
    return lax.axis_index("rows") & 1


def row_coefficients(upper, lower, gates, inverse, bias, h, decay, drive):
    half = upper.shape[0]
    values = jnp.where(h < half, upper[h & (half - 1)], lower[h & (half - 1)])
    root = rate_root(gates[pl.ds(h, 1), :], bias)
    root = root.reshape(values.shape)
    force = root * (values * inverse[pl.ds(h, 1), :])
    every = slice(None)
    widen(decay, (h, every, every), tiles_of(1.0 - root * root))
    widen(drive, (h, every, every), tiles_of(force))


def put_taps(taps, first, last):
    for k, tap in enumerate(edge_masked(first, last)):
        widen(taps, (k, slice(None)), tiles_of(tap))


def half_line(core, half):
    size = half.shape[2]
    return pl.ds(pl.multiple_of(core * size, LANES), size)


def near_side(p0, p1, p2, p3, q0, q1, q2, q3, upper, lower, bias, near_taps, far_taps, far_gate, inverse, raw, decay, drive, kept, end, raw_half, far_raw):
    core, x = place()
    odd = parity()
    rows = raw.shape[1]
    near, far = odd * 3, 3 - odd * 3
    for other, pieces in ((0, (p0, p1, p2, p3)), (1, (q0, q1, q2, q3))):
        for s, piece in enumerate(pieces):
            at = lane_tile(core ^ other, x + s)
            for k in range(3):
                raw[k, :, at] = piece[near + k]
            for k in range(2):
                far_raw[k, :, at] = piece[far + k]
            far_gate[:, at] = piece[far + 2]
            inverse[:, at] = piece[6]
    raw_half[...] = raw[:, :, half_line(core, raw_half)]
    put_taps(near_taps, raw[0], raw[1])
    put_taps(far_taps, far_raw[0], far_raw[1])
    bias_column = bias[:, :1]
    gates = raw.at[2]

    def step(r, state):
        h1, h2 = (row_at(2 * r + k, odd == 1, rows) for k in range(2))
        for h in (h1, h2):
            row_coefficients(upper, lower, gates, inverse, bias_column, h, decay, drive)
        middle, state = two_rows(state, h1, h2, decay, drive, near_taps)
        put(kept, h1, middle)
        put(kept, h2, state)
        return state

    state = tiles_of(jnp.zeros(end.shape, jnp.float32))
    end[...] = whole(lax.fori_loop(0, rows // 2, step, state, unroll=4))


def far_side(far_gate, inverse, upper, lower, bias, decay, drive):
    bias_column = bias[:, :1]

    def step(h, carry):
        row_coefficients(upper, lower, far_gate, inverse, bias_column, h, decay, drive)
        return carry

    lax.fori_loop(0, decay.shape[0], step, 0, unroll=4)


def partner_side(first, own_half, other_half, bias, taps, decay, raw):
    core, _ = place()
    _, when = turn()

    @pl.when(when == 1 if first else when > 1)
    def _():
        bias_column = bias[:, :1]
        raw[:, :, half_line(core, own_half)] = own_half[...]
        raw[:, :, half_line(core ^ 1, own_half)] = other_half[...]
        put_taps(taps, raw[0], raw[1])
        every = slice(None)

        def step(h, carry):
            root = rate_root(raw[2, pl.ds(h, 1), :], bias_column)
            line = (1.0 - root * root).reshape(*decay.shape[1:3], raw.shape[2])
            widen(decay, (h, every, every), tiles_of(line))
            return carry

        lax.fori_loop(0, decay.shape[0], step, 0, unroll=4)


def scan_rows(state, upward, decay, drive, taps, emit):
    rows = decay.shape[0]

    def step(r, state):
        h1, h2 = (row_at(2 * r + k, upward, rows) for k in range(2))
        middle, state = two_rows(state, h1, h2, decay, drive, taps)
        if emit is not None:
            emit(h1, middle)
            emit(h2, state)
        return state

    return lax.fori_loop(0, rows // 2, step, state, unroll=rows // 2)


def carried_in(arrived, partner_end, odd, decay, taps):
    state = scan_rows(tiles_of(arrived[...]), odd == 0, decay, None, taps, None)
    return [a + b for a, b in zip(state, tiles_of(partner_end[...]))]


def turn():
    position = lax.axis_index("rows")
    pair, odd = position >> 1, position & 1
    return odd, jnp.where(odd == 1, pair, 3 - pair)


def far_stage(stage, *refs):
    arrived, partner_end = refs[0], refs[1]
    if stage:
        pd, pt, refs = refs[2], refs[3], refs[4:]
    else:
        refs = refs[1:]
    if stage:
        fd, fq, ft, kept_in, leaving_in, kept, leaving = refs
    else:
        fd, fq, ft, kept_in, kept, leaving = refs[1:]
    odd, when = turn()

    @pl.when(when == stage)
    def _():
        if stage:
            state = carried_in(arrived, partner_end, odd, pd, pt)
        else:
            state = tiles_of(arrived[...])
        leaving[...] = whole(scan_rows(state, odd == 0, fd, fq, ft, functools.partial(put, kept)))

    @pl.when(when != stage)
    def _():
        kept[...] = kept_in[...]
        if stage:
            leaving[...] = leaving_in[...]


def last_stage(near_in, far_in, partner_end, pd, pt, fd, fq, ft, nd, nq, nt, kept, out, mixed, made, sems):
    odd, when = turn()
    rows, chans, _ = made.shape

    def copy(h, k):
        return pltpu.make_async_copy(made.at[h], out.at[h], sems.at[k])

    def mix(h, tiles):
        for m, tile in enumerate(tiles):
            at = slice(m * LANES, (m + 1) * LANES)
            mixed[h, :, at] = (kept[h, :, :, at] * tile).reshape(chans, LANES).astype(mixed.dtype)

    def finish(h):
        for m, tile in enumerate(exchanged(tiles_of(mixed[h]))):
            made[h, :, m * LANES : (m + 1) * LANES] = tile
        copy(h, h).start()

    def scan_all(state, upward, decay, drive, taps):
        def pair(r):
            return [row_at(2 * r + k, upward, rows) for k in range(2)]

        def advance(r, state):
            middle, state = two_rows(state, *pair(r), decay, drive, taps)
            for h, tiles in zip(pair(r), (middle, state)):
                mix(h, tiles)
            return state

        def step(r, state):
            for h in pair(r - 1):
                finish(h)
            return advance(r, state)

        lax.fori_loop(1, rows // 2, step, advance(0, state))
        for h in pair(rows // 2 - 1):
            finish(h)

    @pl.when(when == 3)
    def _():
        scan_all(carried_in(far_in, partner_end, odd, pd, pt), odd == 0, fd, fq, ft)

    @pl.when(when != 3)
    def _():
        scan_all(tiles_of(near_in[...]), odd == 1, nd, nq, nt)

    for k in range(rows):
        copy(k, k).wait()


def chan_shift(value, target):
    return lax.ppermute(value, "chan", [(i, target(i)) for i in range(32)])


def along_x(value, s):
    return chan_shift(value, lambda i: (i & ~6) | ((((i >> 1) + s) & 3) << 1))


def along_y(value, s):
    return chan_shift(value, lambda i: (i & 7) | ((((i >> 3) + s) & 3) << 3))


def other_core(value):
    return chan_shift(value, lambda i: i ^ 1)


def shards(feats, norm_gain, proj_weight, chan_bias):
    rows, chans, cols = feats.shape
    gain, bias = norm_gain.reshape(1, chans), chan_bias.reshape(1, chans)
    piece = f32(SLOTS, rows, LANES)
    half = f32(4, SLOTS, rows, LANES)
    column = f32(chans, LANES)
    arguments = (feats, gain, proj_weight, bias)
    keep, send, feats, gain, bias = pl.pallas_call(
        project,
        out_shape=(half, half, jax.ShapeDtypeStruct(feats.shape, feats.dtype), column, column),
        in_specs=[pl.BlockSpec(memory_space=pltpu.HBM)] * 4,
        out_specs=(VMEM,) * 5,
        scratch_shapes=[
            pltpu.VMEM(gain.shape, gain.dtype),
            pltpu.VMEM(proj_weight.shape, proj_weight.dtype),
            pltpu.VMEM(bias.shape, bias.dtype),
            pltpu.VMEM((18 * rows, rows * chans), jnp.bfloat16),
            pltpu.VMEM((TILES, SLOTS * rows, LANES), jnp.float32),
            pltpu.SemaphoreType.DMA((3 + rows // CHUNK,)),
        ],
        compiler_params=pltpu.CompilerParams(vmem_limit_bytes=24 << 20),
    )(*(pltpu.with_memory_space_constraint(v, pltpu.HBM) for v in arguments))
    block = f32(rows, chans // 8, 8, cols)
    rows_half = f32(rows // 2, chans // 8, 8, cols)
    gained = [call(functools.partial(weave_rows, at), rows_half, feats, gain) for at in (0, rows // 2)]
    mine, *others = call(join_cores, (piece,) * 4, keep, other_core(send))
    part = call(join_x, piece, mine, *(along_x(v, s + 1) for s, v in enumerate(others)))
    part, gained[0] = lax.optimization_barrier((part, gained[0]))
    whole = call(join_y, piece, part, *(along_y(part, s) for s in (3, 2, 1)))
    whole, gained[1] = lax.optimization_barrier((whole, gained[1]))
    pieces = [whole] + [along_x(whole, s) for s in (3, 2, 1)]
    pieces = pieces + [other_core(v) for v in pieces]

    state = f32(chans // 8, 8, cols)
    wider = f32(rows, chans // 8, 8, cols + 2 * LANES)
    taps = f32(3, rows, cols + 2 * LANES)
    line, lines = f32(rows, cols), f32(3, rows, cols)
    near_taps, far_taps, far_gate, inverse, _, near_decay, near_drive, kept, end, raw_half = pl.pallas_call(
        near_side,
        out_shape=(taps, taps, line, line, lines, wider, wider, block, state, f32(3, rows, cols // 2)),
        in_specs=[VMEM] * 11,
        out_specs=(VMEM,) * 10,
        scratch_shapes=[pltpu.VMEM((2, rows, cols), jnp.float32)],
        compiler_params=pltpu.CompilerParams(vmem_limit_bytes=24 << 20),
    )(*pieces, *gained, bias)

    def along_rows(value, pairs):
        return lax.ppermute(value, "rows", pairs)

    swap = [(p, p ^ 1) for p in range(8)]
    partner_end = along_rows(end, swap)
    far_decay, far_drive = call(far_side, (wider, wider), far_gate, inverse, *gained, bias)
    far = (far_decay, far_drive, far_taps)
    own_half = along_rows(raw_half, swap)
    other_half = other_core(own_half)
    kept, leaving = call(
        functools.partial(far_stage, 0), (block, state), partner_end, partner_end, *far, kept, aliases={5: 0}
    )
    for stage, pairs in ((1, FIRST_HOP), (2, SECOND_HOP)):
        arrived = along_rows(leaving, pairs)
        if stage == 2:
            leaving, own_half = lax.optimization_barrier((leaving, own_half))
        partner_taps, partner_decay = pl.pallas_call(
            functools.partial(partner_side, stage == 1),
            out_shape=(taps, wider),
            in_specs=[VMEM] * 3,
            out_specs=(VMEM,) * 2,
            scratch_shapes=[pltpu.VMEM((3, rows, cols), jnp.float32)],
            compiler_params=pltpu.CompilerParams(vmem_limit_bytes=24 << 20),
        )(own_half, other_half, bias)
        partner = (partner_end, partner_decay, partner_taps)
        kept, leaving = call(
            functools.partial(far_stage, stage), (block, state), arrived, *partner, *far, kept, leaving,
            aliases={7: 0, 8: 1},
        )
    near_in = along_rows(leaving, LAST_PAIRS)
    far_in = along_rows(leaving, THIRD_HOP)
    return pl.pallas_call(
        last_stage,
        out_shape=jax.ShapeDtypeStruct(feats.shape, jnp.bfloat16),
        in_specs=[VMEM] * 12,
        out_specs=pl.BlockSpec(memory_space=pl.ANY),
        scratch_shapes=[
            pltpu.VMEM(feats.shape, jnp.bfloat16),
            pltpu.VMEM(feats.shape, jnp.bfloat16),
            pltpu.SemaphoreType.DMA((rows,)),
        ],
        compiler_params=pltpu.CompilerParams(vmem_limit_bytes=24 << 20),
    )(near_in, far_in, *partner, *far, near_decay, near_drive, near_taps, kept)


def solution(mesh):
    in_specs = (P("rows", "chan", None), P("chan"), P(None, "chan"), P("chan"))
    out_specs = P("rows", "chan", None)
    return jax.shard_map(shards, mesh=mesh, in_specs=in_specs, out_specs=out_specs, check_vma=False)
```
